32 devices in a mesh: mod: 4 (over z), tok: 8 (over y, x, core).
Axes of the slice: x: 2, y: 2, z: 4, core: 2. Of those that a mesh axis runs over, the one named last changes fastest.
Arguments:
- tokens: bfloat16 [8, 4096, 1024], P('mod', 'tok'), may hold values from -8 to 8
- kind_ids: int32 [8, 4096], P('mod', 'tok'), may hold values from 0 to 3
- kind_table: bfloat16 [8, 4, 1024], P('mod'), may hold values from -3 to 3
- present: int32 [8, 4096], P('mod', 'tok'), may hold values from 0 to 1, as said below
- lengths: int32 [8], P('mod'), may hold values from 512 to 4096, as said below
- latents: bfloat16 [8, 512, 1024], P('mod', 'tok'), may hold values from -288 to 288
- w_key: bfloat16 [8, 1024, 1024], P('mod'), may hold values from -0.1875 to 0.1875
- w_value: bfloat16 [8, 1024, 1024], P('mod'), may hold values from -0.1875 to 0.1875
- w_dquery: bfloat16 [8, 1024, 1024], P('mod'), may hold values from -0.375 to 0.375
- w_unite: bfloat16 [8, 1024, 1024], P('mod'), may hold values from -0.0625 to 0.0625
Outputs:
- decoded: bfloat16 [8, 4096, 1024], P('mod', 'tok')
- losses: float32 [8], P('mod')
The draws below stay inside these ranges and needn't reach their ends.
Inputs may be any that keep to these rules, and one draw needn't show every extreme that they name: The first token of every group is present. `lengths`: some group has length 4096.
All inputs are finite; a program needn't handle non-finite values.
Results may differ from the reference program's by a relative error of at most 0.018.
The reference program's roundings to bfloat16 on the way (of `hidden`, `weights`, `united`, `dquery` and `probs`) count: a program that leaves them out, or rounds other values in their place, can miss the bound.
Values may be sent and summed in bfloat16 or wider, within the bound.
No kernel may reach another device: no remote copies, remote signals or barrier semaphores. Data moves between devices by JAX's collectives and lax.ppermute only.
A program may use at most 128 MiB of HBM per device.

```python
import math
import jax
import jax.numpy as jnp
from jax import lax

D = 1024
HEADS = 8
LAT = 512
KINDS = 4
GROUPS = 8
SEQ = 4096


def draw_tokens(key, part):
    ramp = jnp.arange(SEQ, dtype=jnp.float32)[None, :, None] / SEQ
    entries = jnp.clip(jax.random.normal(jax.random.fold_in(key, 41), (GROUPS, SEQ, D), jnp.float32), -4.0, 4.0)
    scale = 0.5 * (1.0 + 3.0 * ramp)
    return (entries * scale).astype(jnp.bfloat16)


def draw_present(key, part):
    coins = jax.random.randint(jax.random.fold_in(key, 11), (GROUPS, SEQ), 0, 4)
    marks = (coins < 3).astype(jnp.int32)
    first = (jnp.arange(SEQ, dtype=jnp.int32) == 0)[None, :]
    return jnp.where(first, 1, marks).astype(jnp.int32)


def draw_lengths(key, part):
    spans = jax.random.randint(jax.random.fold_in(key, 21), (GROUPS,), SEQ // 8, SEQ + 1)
    chosen = jax.random.randint(jax.random.fold_in(key, 22), (), 0, GROUPS)
    return jnp.where(jnp.arange(GROUPS, dtype=jnp.int32) == chosen, SEQ, spans).astype(jnp.int32)


def draw_latents(key, part):
    offsets = jax.random.randint(jax.random.fold_in(key, 31), (GROUPS, 1), 0, 32)
    row_index = jnp.arange(LAT, dtype=jnp.int32)[None, :]
    planted = (row_index + offsets) % 32 == 0
    logscale = jax.random.uniform(jax.random.fold_in(key, 32), (GROUPS, LAT, 1), jnp.float32, math.log(3.0), math.log(6.0))
    entries = jnp.clip(jax.random.normal(jax.random.fold_in(key, 33), (GROUPS, LAT, D), jnp.float32), -3.0, 3.0)
    boost = jnp.where(planted, 16.0, 1.0).astype(jnp.float32)[:, :, None]
    return (entries * jnp.exp(logscale) * boost).astype(jnp.bfloat16)


def set_ends(array, own_key, smallest, top_value):
    longest = array.shape.index(max(array.shape))
    spots = []
    for shift in (0, 1):
        where = [jax.random.randint(jax.random.fold_in(own_key, axis), (), 0, length) for axis, length in enumerate(array.shape)]
        where[longest] = (where[longest] + shift) % array.shape[longest]
        spots.append(tuple(where))
    return array.at[spots[0]].set(smallest).at[spots[1]].set(top_value)


def steps_of(key, extent, cuts, smallest, top_value):
    gain, own = 1.0, jax.random.fold_in(key, 6)
    for axis_at, shards_of in cuts:
        steps = jnp.exp(jax.random.uniform(jax.random.fold_in(own, axis_at), (shards_of,), jnp.float32, smallest / len(cuts), top_value / len(cuts)))
        gain = gain * jnp.repeat(steps, extent[axis_at] // shards_of).reshape([-1 if axis == axis_at else 1 for axis in range(len(extent))])
    return gain


def gaussian(rng, extent, scale, reach, cuts=(), held_as=jnp.bfloat16):
    drawn = scale * jax.random.normal(rng, extent, jnp.float32)
    if cuts:
        drawn = drawn * steps_of(rng, extent, cuts, -0.22, 0.18)
    return jnp.clip(drawn, -reach, reach).astype(held_as)


def setup_inputs(seed: int = 0) -> dict:
    arg_keys = jax.random.split(jax.random.key(seed), 11)
    return {
        "tokens": draw_tokens(jax.random.fold_in(arg_keys[10], 71), 0),
        "kind_ids": set_ends(jax.random.randint(arg_keys[1], (GROUPS, SEQ), 0, KINDS), jax.random.fold_in(arg_keys[1], 1), 0, KINDS - 1).astype(jnp.int32),
        "kind_table": gaussian(arg_keys[2], (GROUPS, KINDS, D), 0.5, 3.0, ((0, 4),)),
        "present": draw_present(jax.random.fold_in(arg_keys[10], 71), 0),
        "lengths": draw_lengths(jax.random.fold_in(arg_keys[10], 71), 0),
        "latents": draw_latents(jax.random.fold_in(arg_keys[10], 71), 0),
        "w_key": gaussian(arg_keys[6], (GROUPS, D, D), D ** -0.5, 0.1875, ((0, 4),)),
        "w_value": gaussian(arg_keys[7], (GROUPS, D, D), D ** -0.5, 0.1875, ((0, 4),)),
        "w_dquery": gaussian(arg_keys[8], (GROUPS, D, D), (D // 4) ** -0.5, 0.375, ((0, 4),)),
        "w_unite": gaussian(arg_keys[9], (GROUPS, D, D), (GROUPS * D) ** -0.5, 0.0625, ((0, 4),)),
    }


def encode_group(hidden, latent, wkey, wvalue, valid):
    keys = jnp.dot(hidden, wkey, preferred_element_type=jnp.float32).astype(jnp.bfloat16)
    values = jnp.dot(hidden, wvalue, preferred_element_type=jnp.float32).astype(jnp.bfloat16)
    head_dim = D // HEADS
    qhead = latent.reshape(LAT, HEADS, head_dim).transpose(1, 0, 2)
    khead = keys.reshape(SEQ, HEADS, head_dim).transpose(1, 0, 2)
    vhead = values.reshape(SEQ, HEADS, head_dim).transpose(1, 0, 2)

    def one_head(trio):
        qpart, kpart, vpart = trio
        scores = jnp.dot(qpart, kpart.T, preferred_element_type=jnp.float32) / math.sqrt(head_dim)
        masked = jnp.where(valid[None, :], scores, -1e+30)
        top = lax.optimization_barrier(jnp.max(masked, axis=-1, keepdims=True))
        weights = jnp.where(valid[None, :], jnp.exp(masked - top), 0.0)
        denom = lax.optimization_barrier(jnp.sum(weights, axis=-1, keepdims=True))
        numer = jnp.dot(weights.astype(jnp.bfloat16), vpart, preferred_element_type=jnp.float32)
        return numer / denom
    pooled = lax.map(one_head, (qhead, khead, vhead))
    return pooled.transpose(1, 0, 2).reshape(LAT, D)

def decode_group(dquery, united):
    head_dim = D // HEADS
    block = math.gcd(SEQ, 4096)
    fhead = united.reshape(LAT, HEADS, head_dim).astype(jnp.float32)

    def one_block(rows):
        qrows = rows.reshape(block, HEADS, head_dim).astype(jnp.float32)
        scores = jnp.einsum('bhe,lhe->bhl', qrows, fhead) / math.sqrt(head_dim)
        probs = jax.nn.softmax(scores, axis=-1).astype(jnp.bfloat16)
        out = jnp.einsum('bhl,lhe->bhe', probs.astype(jnp.float32), fhead)
        return out.astype(jnp.bfloat16).reshape(block, D)
    return lax.map(one_block, dquery.reshape(SEQ // block, block, D)).reshape(SEQ, D)

def reference(tokens, kind_ids, kind_table, present, lengths, latents, w_key, w_value, w_dquery, w_unite):
    position = jnp.arange(SEQ, dtype=jnp.int32)
    hiddens = []
    valids = []
    unite_pre = jnp.zeros((LAT, D), jnp.float32)
    for group in range(GROUPS):
        onehot = (kind_ids[group][:, None] == jnp.arange(KINDS, dtype=jnp.int32)[None, :]).astype(jnp.float32)
        added = jnp.dot(onehot, kind_table[group].astype(jnp.float32))
        hidden = (tokens[group].astype(jnp.float32) + added).astype(jnp.bfloat16)
        valid = (present[group] == 1) & (position < lengths[group])
        pooled = encode_group(hidden, latents[group], w_key[group], w_value[group], valid)
        unite_pre = unite_pre + jnp.dot(pooled.astype(jnp.bfloat16), w_unite[group], preferred_element_type=jnp.float32)
        hiddens.append(hidden)
        valids.append(valid)
    united = jax.nn.gelu(unite_pre, approximate=False).astype(jnp.bfloat16)
    outputs = []
    losses = []
    for group in range(GROUPS):
        dquery = jnp.dot(hiddens[group], w_dquery[group], preferred_element_type=jnp.float32).astype(jnp.bfloat16)
        decoded = decode_group(dquery, united)
        diff = decoded.astype(jnp.float32) - tokens[group].astype(jnp.float32)
        err_row = lax.optimization_barrier(jnp.mean(diff * diff, axis=-1))
        err = jnp.sum(jnp.where(valids[group], err_row, 0.0))
        count = jnp.sum(valids[group].astype(jnp.float32))
        outputs.append(decoded)
        losses.append(err / count)
    return (jnp.stack(outputs), jnp.stack(losses))
```

```python
import functools
import math

import jax
import jax.numpy as jnp
from jax import lax
from jax.experimental import pallas as pl
from jax.experimental.pallas import tpu as pltpu
from jax.sharding import PartitionSpec as P

HEADS = 8
MASKED = -1e30
FLAG = 256
BF16 = jnp.bfloat16
F32 = jnp.float32


def nt_dot(a, b):
    return lax.dot_general(a, b, (((1,), (1,)), ((), ())), preferred_element_type=F32)


def split3(x):
    hi = x.astype(BF16)
    rest = x - hi.astype(F32)
    mid = rest.astype(BF16)
    low = (rest - mid.astype(F32)).astype(BF16)
    return hi.astype(F32), mid.astype(F32), low.astype(F32)


def project_kernel(idx, tok, meta, table, wk, wv, wd, key, val, dq, hid):
    @pl.when(pl.program_id(0) == 0)
    def _():
        kinds = table.shape[0]
        ids = meta[...] & (FLAG - 1)
        row = lax.broadcasted_iota(jnp.int32, (kinds, ids.shape[1]), 0)
        onehot = (row == ids).astype(F32).astype(BF16)
        added = lax.dot_general(
            onehot, table[...], (((0,), (0,)), ((), ())), preferred_element_type=F32
        )
        hid[...] = (tok[...].astype(F32) + added).astype(BF16)

    h = hid[...]
    for w, out in ((wk, key), (wv, val), (wd, dq)):
        out[...] = jnp.dot(h, w[...], preferred_element_type=F32).astype(BF16)


def project(idx, tok, meta, table, wk, wv, wd):
    rows, width = tok.shape[1:]
    kinds = table.shape[1]
    block = min(256, width)
    wspec = pl.BlockSpec((None, width, block), lambda j, idx: (idx[1], 0, j))
    ospec = pl.BlockSpec((rows, block), lambda j, idx: (0, j))
    out = jax.ShapeDtypeStruct((rows, width), BF16)
    return pl.pallas_call(
        project_kernel,
        grid_spec=pltpu.PrefetchScalarGridSpec(
            num_scalar_prefetch=1,
            grid=(width // block,),
            in_specs=[
                pl.BlockSpec((None, rows, width), lambda j, idx: (idx[0], 0, 0)),
                pl.BlockSpec((1, rows), lambda j, idx: (0, 0)),
                pl.BlockSpec((None, kinds, width), lambda j, idx: (idx[1], 0, 0)),
                wspec,
                wspec,
                wspec,
            ],
            out_specs=[ospec] * 3,
            scratch_shapes=[pltpu.VMEM((rows, width), BF16)],
        ),
        out_shape=[out] * 3,
        cost_estimate=pl.CostEstimate(
            flops=6 * rows * width * width,
            bytes_accessed=6 * width * width + 8 * rows * width,
            transcendentals=0,
        ),
        name="project",
    )(idx, tok, meta, table, wk, wv, wd)


def pool_kernel(chips, head_dim, *refs):
    q_refs = refs[: 2 * chips]
    k0, k1, v0, v1, meta0, meta1 = refs[2 * chips : 2 * chips + 6]
    outs = refs[2 * chips + 6 : 3 * chips + 6]
    stats = refs[3 * chips + 6 :]
    h = pl.program_id(0)
    c = math.log2(math.e) / math.sqrt(head_dim)
    k = jnp.concatenate([k0[...], k1[...]], axis=0)
    v = jnp.concatenate([v0[...], v1[...]], axis=0)
    v = jnp.concatenate([v, jnp.ones_like(v)], axis=1)
    meta = jnp.concatenate([meta0[...], meta1[...]], axis=1)
    bias = jnp.where(meta >= FLAG, 0.0, MASKED)
    for j in range(chips):
        q = jnp.concatenate([q_refs[2 * j][...], q_refs[2 * j + 1][...]], axis=0)
        s = nt_dot(q, k) + bias
        top = jnp.max(s, axis=1, keepdims=True)
        p = jnp.exp2((s - top) * c).astype(BF16)
        o = jnp.dot(p, v, preferred_element_type=F32)
        numer, denom = o[:, :head_dim], o[:, head_dim:]
        out = outs[j]
        out[:, pl.ds(pl.multiple_of(h * head_dim, head_dim), head_dim)] = numer.astype(out.dtype)
        lane = lax.broadcasted_iota(jnp.int32, denom.shape, 1)
        st = stats[j][...]
        parts = split3(jnp.broadcast_to(top, denom.shape)) + split3(denom)
        for i, part in enumerate(parts):
            st = jnp.where(lane == i * HEADS + h, part, st)
        stats[j][...] = st

        @pl.when(h == HEADS - 1)
        def _():
            out[:, HEADS * head_dim :] = st.astype(out.dtype)


def pool(qs, keys, vals, metas, chips):
    rows, width = qs[0].shape
    head_dim = width // HEADS
    seq = keys[0].shape[0]
    col = lambda n: pl.BlockSpec((n, head_dim), lambda h: (0, h))
    full = pl.BlockSpec((2 * rows, width + head_dim), lambda h: (0, 0))
    lat = 2 * rows * chips
    return pl.pallas_call(
        functools.partial(pool_kernel, chips, head_dim),
        grid=(HEADS,),
        in_specs=[col(rows)] * (2 * chips)
        + [col(seq)] * 4
        + [pl.BlockSpec((1, seq), lambda h: (0, 0))] * 2,
        out_specs=[full] * chips,
        out_shape=[
            jax.ShapeDtypeStruct((2 * rows, width + head_dim), F32 if j == 0 else BF16)
            for j in range(chips)
        ],
        scratch_shapes=[pltpu.VMEM((2 * rows, head_dim), F32)] * chips,
        cost_estimate=pl.CostEstimate(
            flops=12 * lat * 2 * seq * width,
            bytes_accessed=2 * (2 * lat * width + 4 * seq * width),
            transcendentals=lat * 2 * seq * HEADS,
        ),
        name="pool",
    )(*qs, *keys, *vals, *metas)


def unite_kernel(chips, head_dim, idx, *refs):
    parts = refs[:chips]
    w, same, other, pooled = refs[chips:]
    width = HEADS * head_dim
    rows = same.shape[0]

    @pl.when(pl.program_id(0) == 0)
    def _():
        c = math.log2(math.e) / math.sqrt(head_dim)
        stats = [part[:, width:].astype(F32) for part in parts]
        for h in range(HEADS):
            pick = lambda st, i: st[:, i * HEADS + h : i * HEADS + h + 1]
            tops = [pick(st, 0) + pick(st, 1) + pick(st, 2) for st in stats]
            dens = [pick(st, 3) + pick(st, 4) + pick(st, 5) for st in stats]
            top = functools.reduce(jnp.maximum, tops)
            scale = [jnp.exp2((t - top) * c) for t in tops]
            denom = sum(s * d for s, d in zip(scale, dens))
            cols = pl.ds(h * head_dim, head_dim)
            numer = sum(s * part[:, cols].astype(F32) for s, part in zip(scale, parts))
            pooled[:, cols] = (numer / denom).astype(BF16)

    t = jnp.dot(pooled[...], w[...], preferred_element_type=F32)
    same[...] = t[:rows]
    other[...] = t[rows:].astype(BF16)


def unite(idx, parts, w):
    rows = parts[0].shape[0] // 2
    width = w.shape[1]
    head_dim = width // HEADS
    block = min(256, width)
    ospec = pl.BlockSpec((rows, block), lambda j, idx: (0, j))
    return pl.pallas_call(
        functools.partial(unite_kernel, len(parts), head_dim),
        grid_spec=pltpu.PrefetchScalarGridSpec(
            num_scalar_prefetch=1,
            grid=(width // block,),
            in_specs=[pl.BlockSpec(parts[0].shape, lambda j, idx: (0, 0))] * len(parts)
            + [pl.BlockSpec((None, width, block), lambda j, idx: (idx[1], 0, j))],
            out_specs=[ospec, ospec],
            scratch_shapes=[pltpu.VMEM((2 * rows, width), BF16)],
        ),
        out_shape=[
            jax.ShapeDtypeStruct((rows, width), F32),
            jax.ShapeDtypeStruct((rows, width), BF16),
        ],
        name="unite",
    )(idx, *parts, w)


def cut_kernel(zs, idx, a, b, *outs):
    block = outs[0].shape[1]
    for j in range(zs):
        cols = pl.ds(pl.multiple_of((idx[0] ^ j) * block, block), block)
        outs[j][...] = (a[:, cols] + b[:, cols].astype(F32)).astype(outs[j].dtype)


def cut(z, a, b, zs):
    rows, width = a.shape
    block = width // zs
    full = pl.BlockSpec((rows, width), lambda i, idx: (0, 0))
    return pl.pallas_call(
        functools.partial(cut_kernel, zs),
        grid_spec=pltpu.PrefetchScalarGridSpec(
            num_scalar_prefetch=1,
            grid=(1,),
            in_specs=[full, full],
            out_specs=[pl.BlockSpec((rows, block), lambda i, idx: (0, 0))] * zs,
        ),
        out_shape=[
            jax.ShapeDtypeStruct((rows, block), F32 if j == 0 else BF16) for j in range(zs)
        ],
        name="cut",
    )(z, a, b)


def join_kernel(zs, idx, *refs):
    out = refs[zs]
    block = refs[0].shape[1]
    for j in range(zs):
        cols = pl.ds(pl.multiple_of((idx[0] ^ j) * block, block), block)
        out[:, cols] = refs[j][...]


def join(z, pieces):
    zs = len(pieces)
    rows, block = pieces[0].shape
    return pl.pallas_call(
        functools.partial(join_kernel, zs),
        grid_spec=pltpu.PrefetchScalarGridSpec(
            num_scalar_prefetch=1,
            grid=(1,),
            in_specs=[pl.BlockSpec((rows, block), lambda i, idx: (0, 0))] * zs,
            out_specs=pl.BlockSpec((rows, zs * block), lambda i, idx: (0, 0)),
        ),
        out_shape=jax.ShapeDtypeStruct((rows, zs * block), BF16),
        name="join",
    )(z, *pieces)


def decode_kernel(n_u, head_dim, idx, dq, tok, meta, base, *refs):
    u_refs = refs[:n_u]
    out, err, acc = refs[n_u:]
    h = pl.program_id(0)
    c = math.log2(math.e) / math.sqrt(head_dim)
    u = jnp.concatenate([r[...] for r in u_refs], axis=0)
    uu = jnp.concatenate([u, jnp.ones_like(u)], axis=1)
    rows = dq.shape[0]
    step = min(128, rows)
    for r in range(0, rows, step):
        band = pl.ds(r, step)
        s = nt_dot(dq[band, :], u)
        top = jnp.max(s, axis=1, keepdims=True)
        p = jnp.exp2((s - top) * c).astype(BF16)
        o = jnp.dot(p, uu, preferred_element_type=F32)
        dec = (o[:, :head_dim] / o[:, head_dim:]).astype(BF16)
        out[band, :] = dec
        diff = dec.astype(F32) - tok[band, :].astype(F32)
        sq = diff * diff

        @pl.when(h == 0)
        def _():
            acc[band, :] = sq

        @pl.when(h > 0)
        def _():
            acc[band, :] += sq

    @pl.when(h == HEADS - 1)
    def _():
        valid = jnp.broadcast_to((meta[...] >= FLAG).astype(F32), (8, rows))
        total = jnp.dot(
            valid, acc[...], precision=lax.Precision.HIGHEST, preferred_element_type=F32
        )
        total = jnp.sum(total, axis=1, keepdims=True) * (1.0 / (HEADS * head_dim))
        err[...] = base[...] + jnp.broadcast_to(total, err.shape)


def decode(idx, groups, dq, tok, meta, base, us):
    rows, width = dq.shape
    head_dim = width // HEADS
    n_u = len(us)
    small = pl.BlockSpec((8, head_dim), lambda h, idx: (0, 0))
    lat = n_u * us[0].shape[0]
    return pl.pallas_call(
        functools.partial(decode_kernel, n_u, head_dim),
        grid_spec=pltpu.PrefetchScalarGridSpec(
            num_scalar_prefetch=1,
            grid=(HEADS,),
            in_specs=[
                pl.BlockSpec((rows, head_dim), lambda h, idx: (0, h)),
                pl.BlockSpec((None, rows, head_dim), lambda h, idx: (idx[0], 0, h)),
                pl.BlockSpec((1, rows), lambda h, idx: (0, 0)),
                small,
            ]
            + [pl.BlockSpec((u.shape[0], head_dim), lambda h, idx: (0, h)) for u in us],
            out_specs=[
                pl.BlockSpec((None, rows, head_dim), lambda h, idx: (idx[0], 0, h)),
                small,
            ],
            scratch_shapes=[pltpu.VMEM((rows, head_dim), F32)],
        ),
        out_shape=[
            jax.ShapeDtypeStruct((groups, rows, width), BF16),
            jax.ShapeDtypeStruct((8, head_dim), F32),
        ],
        cost_estimate=pl.CostEstimate(
            flops=6 * rows * lat * width,
            bytes_accessed=6 * rows * width,
            transcendentals=rows * lat * HEADS,
        ),
        name="decode",
    )(idx, dq, tok, meta, base, *us)


def per_device(
    nt, zs, tokens, kind_ids, kind_table, present, lengths, latents, w_key, w_value, w_dquery, w_unite
):
    groups, rows, width = tokens.shape
    head_dim = width // HEADS
    chips = nt // 2
    t = lax.axis_index("tok")
    z = lax.axis_index("mod").astype(jnp.int32)
    core = (t % 2).astype(jnp.int32)
    swap = lambda x, k: lax.ppermute(x, "tok", [(i, i ^ k) for i in range(nt)])
    swap_z = lambda x, k: lax.ppermute(x, "mod", [(i, i ^ k) for i in range(zs)])
    own = lambda x: lax.dynamic_index_in_dim(x, core, 0, keepdims=True)
    alien = lambda x: lax.dynamic_index_in_dim(x, 1 - core, 0, keepdims=True)

    lat_own, lat_alien = own(latents)[0], alien(latents)[0]
    far_first = sorted(range(nt), key=lambda k: -bin(k).count("1"))
    got = {k: (swap(lat_alien if k % 2 else lat_own, k) if k else lat_own) for k in far_first}
    qs = [got[k] for k in range(nt)]

    position = t * rows + jnp.arange(rows, dtype=jnp.int32)
    valid = (present == 1) & (position[None, :] < lengths[:, None])
    meta = kind_ids + FLAG * valid.astype(jnp.int32)
    metas = [own(meta), swap(alien(meta), 1)]
    tok_alien = swap(alien(tokens), 1)
    idx_own = jnp.stack([core, core])
    idx_alien = jnp.stack([jnp.zeros_like(core), core])
    kvd = [
        project(idx_own, tokens, metas[0], kind_table, w_key, w_value, w_dquery),
        project(idx_alien, tok_alien, metas[1], kind_table, w_key, w_value, w_dquery),
    ]

    sums = pool(qs, [x[0] for x in kvd], [x[1] for x in kvd], metas, chips)
    sums = [s if j == 0 else swap(s, 2 * j) for j, s in enumerate(sums)]
    same, other = unite(idx_own, sums, w_unite)
    other = swap(other, 1)

    pieces = cut(z[None], same, other, zs)
    pieces = [p if j == 0 else swap_z(p, j) for j, p in enumerate(pieces)]
    pre = sum(p.astype(F32) for p in pieces)
    piece = jax.nn.gelu(pre, approximate=False).astype(BF16)
    u = join(z[None], [swap_z(piece, j) if j else piece for j in range(zs)])
    us = [swap(u, 2 * j) if j else u for j in range(chips)]
    us = us + [swap(x, 1) for x in us]

    base = jnp.zeros((8, head_dim), F32)
    dec_alien, err = decode(idx_alien, 1, kvd[1][2], tok_alien, metas[1], base, us)
    dec_back = swap(dec_alien, 1)
    dec, err = decode(idx_own, groups, kvd[0][2], tokens, metas[0], err, us)
    decoded = lax.dynamic_update_index_in_dim(dec, dec_back[0], 1 - core, 0)

    count = sum(jnp.sum((m >= FLAG).astype(F32)) for m in metas)
    count = jnp.broadcast_to(count, (8, head_dim))
    count = sum(swap(count, 2 * j) if j else count for j in range(chips))
    err = sum(swap(err, 2 * j) if j else err for j in range(chips))
    loss = err / count
    loss_alien = swap(loss, 1)
    group = jnp.arange(groups, dtype=jnp.int32)
    losses = jnp.where(group == core, loss[0, 0], loss_alien[0, 0])
    return decoded, losses


def solution(mesh):
    nt, zs = mesh.shape["tok"], mesh.shape["mod"]
    in_specs = (
        P("mod", "tok", None),
        P("mod", "tok"),
        P("mod", None, None),
        P("mod", "tok"),
        P("mod"),
        P("mod", "tok", None),
        P("mod", None, None),
        P("mod", None, None),
        P("mod", None, None),
        P("mod", None, None),
    )
    out_specs = (P("mod", "tok", None), P("mod"))
    return jax.shard_map(
        functools.partial(per_device, nt, zs),
        mesh=mesh,
        in_specs=in_specs,
        out_specs=out_specs,
        check_vma=False,
    )
```

```python
import functools
import math

import jax
import jax.numpy as jnp
from jax import lax
from jax.experimental import pallas as pl
from jax.experimental.pallas import tpu as pltpu
from jax.sharding import PartitionSpec as P

HEADS = 8
MASKED = -1e30
FLAG = 256
BF16 = jnp.bfloat16
F32 = jnp.float32


def nt_dot(a, b):
    return lax.dot_general(a, b, (((1,), (1,)), ((), ())), preferred_element_type=F32)


VMEM = pl.BlockSpec(memory_space=pltpu.VMEM)


def params(mib):
    return pltpu.CompilerParams(vmem_limit_bytes=mib << 20)


def split3(x):
    hi = x.astype(BF16)
    rest = x - hi.astype(F32)
    mid = rest.astype(BF16)
    low = (rest - mid.astype(F32)).astype(BF16)
    return hi.astype(F32), mid.astype(F32), low.astype(F32)


def project_kernel(idx, tok, meta, table, wk, wv, key, val, bias, hid):
    @pl.when(pl.program_id(0) == 0)
    def _():
        kinds, seq = table.shape[0], meta.shape[1]
        ids = meta[...] & (FLAG - 1)
        row = lax.broadcasted_iota(jnp.int32, (kinds, seq), 0)
        onehot = (row == ids).astype(F32).astype(BF16)
        cross = (((0,), (0,)), ((), ()))
        added = lax.dot_general(onehot, table[...], cross, preferred_element_type=F32)
        hid[...] = (tok[...].astype(F32) + added).astype(BF16)
        masked = jnp.where(meta[...] >= FLAG, 0.0, MASKED)
        masked = jnp.broadcast_to(masked, (8, seq)).astype(BF16)
        first = lax.broadcasted_iota(jnp.int32, (8, bias.shape[1]), 0)
        lane = lax.broadcasted_iota(jnp.int32, (8, bias.shape[1]), 1)
        unit = ((first == 0) & (lane == 0)).astype(F32).astype(BF16)
        bias[...] = lax.dot_general(masked, unit, cross, preferred_element_type=F32).astype(BF16)

    h = hid[...]
    for w, out in ((wk, key), (wv, val)):
        out[...] = jnp.dot(h, w[...], preferred_element_type=F32).astype(BF16)


def project(idx, tok, meta, table, wk, wv):
    rows, width = tok.shape[1:]
    kinds = table.shape[1]
    block = min(256, width)
    head_dim = width // HEADS
    wspec = pl.BlockSpec((None, width, block), lambda j, idx: (idx[1], 0, j))
    ospec = pl.BlockSpec((rows, block), lambda j, idx: (0, j))
    full = pl.BlockSpec((rows, width), lambda j, idx: (0, 0))
    out = jax.ShapeDtypeStruct((rows, width), BF16)
    return pl.pallas_call(
        project_kernel,
        grid_spec=pltpu.PrefetchScalarGridSpec(
            num_scalar_prefetch=1,
            grid=(width // block,),
            in_specs=[
                pl.BlockSpec((None, rows, width), lambda j, idx: (idx[0], 0, 0)),
                pl.BlockSpec((1, rows), lambda j, idx: (0, 0)),
                pl.BlockSpec((None, kinds, width), lambda j, idx: (idx[1], 0, 0)),
                wspec,
                wspec,
            ],
            out_specs=[ospec] * 2 + [pl.BlockSpec((rows, head_dim), lambda j, idx: (0, 0)), full],
        ),
        out_shape=[out, out, jax.ShapeDtypeStruct((rows, head_dim), BF16), out],
        compiler_params=params(14),
        cost_estimate=pl.CostEstimate(
            flops=4 * rows * width * width,
            bytes_accessed=4 * width * width + 8 * rows * width,
            transcendentals=0,
        ),
        name="project",
    )(idx, tok, meta, table, wk, wv)


def query_kernel(idx, h0, h1, w, out0, out1):
    for h, out in ((h0, out0), (h1, out1)):
        out[...] = jnp.dot(h[...], w[...], preferred_element_type=F32).astype(BF16)


def query(idx, h0, h1, w):
    rows, width = h0.shape
    block = min(256, width)
    full = pl.BlockSpec((rows, width), lambda j, idx: (0, 0))
    ospec = pl.BlockSpec((rows, block), lambda j, idx: (0, j))
    return pl.pallas_call(
        query_kernel,
        grid_spec=pltpu.PrefetchScalarGridSpec(
            num_scalar_prefetch=1,
            grid=(width // block,),
            in_specs=[full, full, pl.BlockSpec((None, width, block), lambda j, idx: (idx[1], 0, j))],
            out_specs=[ospec] * 2,
        ),
        out_shape=[jax.ShapeDtypeStruct((rows, width), BF16)] * 2,
        compiler_params=params(14),
        cost_estimate=pl.CostEstimate(
            flops=4 * rows * width * width,
            bytes_accessed=2 * width * width + 8 * rows * width,
            transcendentals=0,
        ),
        name="query",
    )(idx, h0, h1, w)


def pool_kernel(n, head_dim, *refs):
    q_refs = refs[: 2 * n]
    k0, k1, v0, v1, b0, b1 = refs[2 * n : 2 * n + 6]
    outs = refs[2 * n + 6 : 3 * n + 6]
    tops, dens = refs[3 * n + 6 :]
    c = math.log2(math.e) / math.sqrt(head_dim)
    rows = 2 * q_refs[0].shape[0]
    lane = lax.broadcasted_iota(jnp.int32, (n * rows, head_dim), 1)
    first = (lane == 0).astype(F32).astype(BF16)

    def one_head(h, carry):
        cols = pl.ds(pl.multiple_of(h * head_dim, head_dim), head_dim)
        bias = jnp.concatenate([b0[...], b1[...]], axis=0)
        k = jnp.concatenate([k0[:, cols], k1[:, cols]], axis=0)
        v = jnp.concatenate([v0[:, cols], v1[:, cols]], axis=0)
        q = jnp.concatenate([r[:, cols] for r in q_refs], axis=0)
        s = nt_dot(jnp.concatenate([q, first], axis=1), jnp.concatenate([k, bias], axis=1))
        top = jnp.max(s, axis=1, keepdims=True)
        p = jnp.exp2((s - top) * c).astype(BF16)
        o = jnp.dot(
            p, jnp.concatenate([v, jnp.ones_like(v)], axis=1), preferred_element_type=F32
        )
        for j, out in enumerate(outs):
            out[:, cols] = o[j * rows : (j + 1) * rows, :head_dim].astype(out.dtype)
        tops[...] = jnp.where(lane == h, top, tops[...])
        dens[...] = jnp.where(lane == h, o[:, head_dim:], dens[...])
        return carry

    lax.fori_loop(0, HEADS, one_head, 0, unroll=2)
    stats = jnp.zeros((n * rows, head_dim), F32)
    for i, part in enumerate(split3(tops[...]) + split3(dens[...])):
        part = jnp.where(lane < HEADS, part, 0.0)
        stats = stats + (pltpu.roll(part, i * HEADS, 1) if i else part)
    for j, out in enumerate(outs):
        out[:, HEADS * head_dim :] = stats[j * rows : (j + 1) * rows].astype(out.dtype)


def pool(qs, keys, vals, biases, owned):
    rows, width = qs[0].shape
    n = len(qs) // 2
    head_dim = width // HEADS
    seq = keys[0].shape[0]
    lat = 2 * rows * n
    return pl.pallas_call(
        functools.partial(pool_kernel, n, head_dim),
        in_specs=[VMEM] * (2 * n + 6),
        out_specs=[VMEM] * n,
        out_shape=[
            jax.ShapeDtypeStruct((2 * rows, width + head_dim), F32 if j in owned else BF16)
            for j in range(n)
        ],
        scratch_shapes=[pltpu.VMEM((lat, head_dim), F32)] * 2,
        compiler_params=params(16),
        cost_estimate=pl.CostEstimate(
            flops=12 * lat * 2 * seq * width,
            bytes_accessed=2 * (2 * lat * width + 4 * seq * width),
            transcendentals=lat * 2 * seq * HEADS,
        ),
        name="pool",
    )(*qs, *keys, *vals, *biases)


def unite_kernel(chips, head_dim, core, *refs):
    parts = refs[:chips]
    w_all, same, other, pooled, w, sems = refs[chips:]
    width = HEADS * head_dim
    bands = sems.shape[0]
    band = width // bands
    copies = []
    for i in range(bands):
        cut = pl.ds(i * band, band)
        copies.append(pltpu.make_async_copy(w_all.at[core[0], cut], w.at[cut], sems.at[i]))
        copies[-1].start()
    rows = same.shape[0]
    c = math.log2(math.e) / math.sqrt(head_dim)
    stats = [part[:, width:].astype(F32) for part in parts]
    for h in range(HEADS):
        pick = lambda st, i: st[:, i * HEADS + h : i * HEADS + h + 1]
        tops = [pick(st, 0) + pick(st, 1) + pick(st, 2) for st in stats]
        dens = [pick(st, 3) + pick(st, 4) + pick(st, 5) for st in stats]
        top = functools.reduce(jnp.maximum, tops)
        scale = [jnp.exp2((t - top) * c) for t in tops]
        denom = sum(s * d for s, d in zip(scale, dens))
        cols = pl.ds(h * head_dim, head_dim)
        numer = sum(s * part[:, cols].astype(F32) for s, part in zip(scale, parts))
        pooled[:, cols] = (numer / denom).astype(BF16)
    for copy in copies:
        copy.wait()
    t = jnp.dot(pooled[...], w[...], preferred_element_type=F32)
    same[...] = t[:rows]
    other[...] = t[rows:].astype(BF16)


def unite(core, parts, w):
    rows = parts[0].shape[0] // 2
    width = w.shape[1]
    return pl.pallas_call(
        functools.partial(unite_kernel, len(parts), width // HEADS),
        in_specs=[pl.BlockSpec(memory_space=pltpu.SMEM)]
        + [VMEM] * len(parts)
        + [pl.BlockSpec(memory_space=pltpu.HBM)],
        out_specs=[VMEM] * 2,
        scratch_shapes=[
            pltpu.VMEM((2 * rows, width), BF16),
            pltpu.VMEM((width, width), BF16),
            pltpu.SemaphoreType.DMA((4,)),
        ],
        out_shape=[
            jax.ShapeDtypeStruct((rows, width), F32),
            jax.ShapeDtypeStruct((rows, width), BF16),
        ],
        compiler_params=params(10),
        name="unite",
    )(core, *parts, w)


def cut_kernel(zs, z, a, b, *outs):
    block = outs[0].shape[1]
    for j in range(zs):
        cols = pl.ds(pl.multiple_of((z[0] ^ j) * block, block), block)
        outs[j][...] = (a[:, cols] + b[:, cols].astype(F32)).astype(outs[j].dtype)


def cut(z, a, b, zs):
    rows, width = a.shape
    return pl.pallas_call(
        functools.partial(cut_kernel, zs),
        in_specs=[pl.BlockSpec(memory_space=pltpu.SMEM), VMEM, VMEM],
        out_specs=[VMEM] * zs,
        out_shape=[
            jax.ShapeDtypeStruct((rows, width // zs), F32 if j == 0 else BF16) for j in range(zs)
        ],
        compiler_params=params(4),
        name="cut",
    )(z, a, b)


def join_kernel(zs, z, *refs):
    out = refs[zs]
    block = refs[0].shape[1]
    for j in range(zs):
        cols = pl.ds(pl.multiple_of((z[0] ^ j) * block, block), block)
        out[:, cols] = refs[j][...]


def join(z, pieces):
    zs = len(pieces)
    rows, block = pieces[0].shape
    return pl.pallas_call(
        functools.partial(join_kernel, zs),
        in_specs=[pl.BlockSpec(memory_space=pltpu.SMEM)] + [VMEM] * zs,
        out_specs=VMEM,
        out_shape=jax.ShapeDtypeStruct((rows, zs * block), BF16),
        compiler_params=params(4),
        name="join",
    )(z, *pieces)


def decode_kernel(n_u, head_dim, dq, tok, meta, base, *refs):
    u_refs = refs[:n_u]
    out, err, acc = refs[n_u:]
    c = math.log2(math.e) / math.sqrt(head_dim)
    rows = dq.shape[0]
    step = min(128, rows)

    def one_head(h, carry):
        cols = pl.ds(pl.multiple_of(h * head_dim, head_dim), head_dim)
        u = jnp.concatenate([r[:, cols] for r in u_refs], axis=0)
        uu = jnp.concatenate([u, jnp.ones_like(u)], axis=1)
        for r in range(0, rows, step):
            band = pl.ds(r, step)
            s = nt_dot(dq[band, cols], u)
            top = jnp.max(s, axis=1, keepdims=True)
            p = jnp.exp2((s - top) * c).astype(BF16)
            o = jnp.dot(p, uu, preferred_element_type=F32)
            dec = (o[:, :head_dim] / o[:, head_dim:]).astype(BF16)
            out[band, cols] = dec
            diff = dec.astype(F32) - tok[band, cols].astype(F32)
            acc[band, :] = jnp.where(h == 0, 0.0, acc[band, :]) + diff * diff
        return carry

    lax.fori_loop(0, HEADS, one_head, 0, unroll=2)
    valid = jnp.broadcast_to((meta[...] >= FLAG).astype(F32), (8, rows))
    total = jnp.dot(valid, acc[...], precision=lax.Precision.HIGHEST, preferred_element_type=F32)
    total = jnp.sum(total, axis=1, keepdims=True) * (1.0 / (HEADS * head_dim))
    count = jnp.sum(valid, axis=1, keepdims=True)
    row = lax.broadcasted_iota(jnp.int32, err.shape, 0)
    err[...] = base[...] + jnp.where(row == 0, total, count)


def decode(dq, tok, meta, base, us):
    rows, width = dq.shape
    head_dim = width // HEADS
    lat = len(us) * us[0].shape[0]
    return pl.pallas_call(
        functools.partial(decode_kernel, len(us), head_dim),
        in_specs=[VMEM] * (4 + len(us)),
        out_specs=[VMEM] * 2,
        scratch_shapes=[pltpu.VMEM((rows, head_dim), F32)],
        out_shape=[
            jax.ShapeDtypeStruct((rows, width), BF16),
            jax.ShapeDtypeStruct((8, head_dim), F32),
        ],
        compiler_params=params(8),
        cost_estimate=pl.CostEstimate(
            flops=6 * rows * lat * width,
            bytes_accessed=6 * rows * width,
            transcendentals=rows * lat * HEADS,
        ),
        name="decode",
    )(dq, tok, meta, base, *us)


def per_device(
    nt, zs, tokens, kind_ids, kind_table, present, lengths, latents, w_key, w_value, w_dquery, w_unite
):
    groups, rows, width = tokens.shape
    head_dim = width // HEADS
    chips = nt // 2
    hbm = lambda x: pltpu.with_memory_space_constraint(x, pltpu.HBM)
    t = lax.axis_index("tok")
    z = lax.axis_index("mod").astype(jnp.int32)
    core = (t % 2).astype(jnp.int32)
    swap = lambda x, k: lax.ppermute(x, "tok", [(i, i ^ k) for i in range(nt)])
    swap_z = lambda x, k: lax.ppermute(x, "mod", [(i, i ^ k) for i in range(zs)])
    own = lambda x: lax.dynamic_index_in_dim(x, core, 0, keepdims=True)
    alien = lambda x: lax.dynamic_index_in_dim(x, 1 - core, 0, keepdims=True)
    far = sorted(range(chips), key=lambda j: -bin(j).count("1"))

    tok_alien = swap(alien(tokens), 1)
    position = t * rows + jnp.arange(rows, dtype=jnp.int32)
    valid = (present == 1) & (position[None, :] < lengths[:, None])
    meta = kind_ids + FLAG * valid.astype(jnp.int32)
    metas = [own(meta), swap(alien(meta), 1)]
    lat_own, lat_alien = own(latents)[0], alien(latents)[0]
    got = {}
    for j in far:
        got[j] = [swap(lat_own, 2 * j) if j else lat_own, swap(lat_alien, 2 * j + 1)]

    idx_own = jnp.stack([core, core])
    idx_alien = jnp.stack([jnp.zeros_like(core), core])
    key0, val0, bias0, hid0 = project(idx_own, hbm(tokens), metas[0], kind_table, hbm(w_key), hbm(w_value))
    key1, val1, bias1, hid1 = project(idx_alien, tok_alien, metas[1], kind_table, hbm(w_key), hbm(w_value))
    dq0, dq1 = query(idx_own, hid0, hid1, hbm(w_dquery))

    near = max(1, chips // 2)
    calls = [[0] + far[: near - 1], [j for j in far[near - 1 :] if j]]
    parts = [None] * chips
    for call in calls:
        if call:
            qs = [x for j in call for x in got[j]]
            owned = [i for i, j in enumerate(call) if j == 0]
            sums = pool(qs, [key0, key1], [val0, val1], [bias0, bias1], owned)
            for j, s in zip(call, sums):
                parts[j] = swap(s, 2 * j) if j else s
    parts[far[-2]], dq0, dq1 = lax.optimization_barrier((parts[far[-2]], dq0, dq1))
    same, other = unite(core[None], parts, hbm(w_unite))
    other = swap(other, 1)

    pieces = cut(z[None], same, other, zs)
    pieces = [p if j == 0 else swap_z(p, j) for j, p in enumerate(pieces)]
    pre = sum(p.astype(F32) for p in pieces)
    piece = jax.nn.gelu(pre, approximate=False).astype(BF16)
    u = join(z[None], [swap_z(piece, j) if j else piece for j in range(zs)])
    us = [swap(u, 2 * j) if j else u for j in range(chips)]
    us = us + [swap(x, 1) for x in us]

    base = jnp.zeros((8, head_dim), F32)
    dec_alien, err = decode(dq1, tok_alien[0], metas[1], base, us)
    dec_back = swap(dec_alien, 1)
    dec, err = decode(dq0, own(tokens)[0], metas[0], err, us)
    group = jnp.arange(groups, dtype=jnp.int32)
    decoded = jnp.where((group == core)[:, None, None], dec[None], dec_back[None])

    err = sum(swap(err, 2 * j) if j else err for j in range(chips))
    err_alien = swap(err, 1)
    losses = jnp.where(group == core, err[0, 0] / err[1, 0], err_alien[0, 0] / err_alien[1, 0])
    return decoded, losses


def solution(mesh):
    nt, zs = mesh.shape["tok"], mesh.shape["mod"]
    in_specs = (
        P("mod", "tok", None),
        P("mod", "tok"),
        P("mod", None, None),
        P("mod", "tok"),
        P("mod"),
        P("mod", "tok", None),
        P("mod", None, None),
        P("mod", None, None),
        P("mod", None, None),
        P("mod", None, None),
    )
    out_specs = (P("mod", "tok", None), P("mod"))
    return jax.shard_map(
        functools.partial(per_device, nt, zs),
        mesh=mesh,
        in_specs=in_specs,
        out_specs=out_specs,
        check_vma=False,
    )
```

```python
import functools
import math

import jax
import jax.numpy as jnp
from jax import lax
from jax.experimental import pallas as pl
from jax.experimental.pallas import tpu as pltpu
from jax.sharding import PartitionSpec as P


HEADS = 8
MASKED = -1e30
FLAG = 256
BF16 = jnp.bfloat16
F32 = jnp.float32


def nt_dot(a, b):
    return lax.dot_general(a, b, (((1,), (1,)), ((), ())), preferred_element_type=F32)


VMEM = pl.BlockSpec(memory_space=pltpu.VMEM)
SMEM = pl.BlockSpec(memory_space=pltpu.SMEM)
HBM = pl.BlockSpec(memory_space=pltpu.HBM)
ANY = pl.BlockSpec(memory_space=pl.ANY)


def params(mib):
    return pltpu.CompilerParams(vmem_limit_bytes=mib << 20)


def split3(x):
    hi = x.astype(BF16)
    rest = x - hi.astype(F32)
    mid = rest.astype(BF16)
    low = (rest - mid.astype(F32)).astype(BF16)
    return hi.astype(F32), mid.astype(F32), low.astype(F32)


def project_kernel(
    core, mine, theirs, meta, kinds_ref, wk, wv, key, val, bias, hid, tok, table, w, tsem, wsem
):
    rows = mine.shape[1]
    seq, width = hid.shape
    bands = wsem.shape[1]
    band = width // bands
    c = core[0]
    loads = [
        pltpu.make_async_copy(src.at[c], tok.at[pl.ds(i * rows, rows)], tsem.at[i])
        for i, src in enumerate((mine, theirs))
    ]
    named = pltpu.make_async_copy(kinds_ref.at[c], table, tsem.at[2])
    named.start()
    loads[0].start()

    def fetch(i, src, j):
        cols = pl.ds(pl.multiple_of(j * band, band), band)
        return pltpu.make_async_copy(src.at[c, :, cols], w.at[i, :, cols], wsem.at[i, j])

    fetch(0, wk, 0).start()
    loads[1].start()
    for j in range(bands):
        for i, src in enumerate((wk, wv)):
            if i or j:
                fetch(i, src, j).start()
    cross = (((0,), (0,)), ((), ()))
    first = lax.broadcasted_iota(jnp.int32, (8, bias.shape[1]), 0)
    lane = lax.broadcasted_iota(jnp.int32, (8, bias.shape[1]), 1)
    unit = ((first == 0) & (lane == 0)).astype(F32).astype(BF16)
    masked = jnp.where(meta[...] >= FLAG, 0.0, MASKED)
    masked = jnp.broadcast_to(masked, (8, seq)).astype(BF16)
    bias[...] = lax.dot_general(masked, unit, cross, preferred_element_type=F32).astype(BF16)
    named.wait()
    kinds = table.shape[0]
    row = lax.broadcasted_iota(jnp.int32, (kinds, seq), 0)
    onehot = (row == (meta[...] & (FLAG - 1))).astype(F32).astype(BF16)
    for i, load in enumerate(loads):
        part = pl.ds(i * rows, rows)
        added = lax.dot_general(
            onehot[:, i * rows : (i + 1) * rows], table[...], cross, preferred_element_type=F32
        )
        load.wait()
        hid[part, :] = (tok[part, :].astype(F32) + added).astype(BF16)

    def one_band(j, carry):
        cols = pl.ds(pl.multiple_of(j * band, band), band)
        for i, (src, out) in enumerate(((wk, key), (wv, val))):
            fetch(i, src, j).wait()
            out[:, cols] = jnp.dot(
                hid[...], w[i, :, cols], preferred_element_type=F32
            ).astype(BF16)
        return carry

    lax.fori_loop(0, bands, one_band, 0)


def project(core, mine, theirs, meta, table, wk, wv):
    rows, width = mine.shape[1:]
    seq = 2 * rows
    bands = max(1, width // 256)
    out = jax.ShapeDtypeStruct((seq, width), BF16)
    return pl.pallas_call(
        project_kernel,
        in_specs=[SMEM, HBM, ANY, VMEM, HBM, HBM, HBM],
        out_specs=[VMEM] * 5,
        out_shape=[out, out, jax.ShapeDtypeStruct((seq, width // HEADS), BF16), out, out],
        scratch_shapes=[
            pltpu.VMEM(table.shape[1:], BF16),
            pltpu.VMEM((2, width, width), BF16),
            pltpu.SemaphoreType.DMA((3,)),
            pltpu.SemaphoreType.DMA((2, bands)),
        ],
        compiler_params=params(16),
        cost_estimate=pl.CostEstimate(
            flops=4 * seq * width * width,
            bytes_accessed=4 * width * width + 4 * seq * width,
            transcendentals=0,
        ),
        name="project",
    )(core, mine, theirs, meta, table, wk, wv)


def query_kernel(core, hid, wd, out, w, sem):
    width = wd.shape[1]
    bands = sem.shape[0]
    band = width // bands

    def fetch(j):
        cols = pl.ds(pl.multiple_of(j * band, band), band)
        return pltpu.make_async_copy(wd.at[core[0], :, cols], w.at[:, cols], sem.at[j])

    for j in range(bands):
        fetch(j).start()

    def one_band(j, carry):
        cols = pl.ds(pl.multiple_of(j * band, band), band)
        fetch(j).wait()
        out[:, cols] = jnp.dot(hid[...], w[:, cols], preferred_element_type=F32).astype(BF16)
        return carry

    lax.fori_loop(0, bands, one_band, 0)


def query(core, hid, wd):
    seq, width = hid.shape
    bands = max(1, width // 256)
    return pl.pallas_call(
        query_kernel,
        in_specs=[SMEM, VMEM, HBM],
        out_specs=VMEM,
        out_shape=jax.ShapeDtypeStruct((seq, width), BF16),
        scratch_shapes=[pltpu.VMEM((width, width), BF16), pltpu.SemaphoreType.DMA((bands,))],
        compiler_params=params(10),
        cost_estimate=pl.CostEstimate(
            flops=2 * seq * width * width,
            bytes_accessed=2 * width * width,
            transcendentals=0,
        ),
        name="query",
    )(core, hid, wd)


def pool_kernel(n, head_dim, *refs):
    q_refs = refs[: 2 * n]
    key, val, bias = refs[2 * n : 2 * n + 3]
    outs = refs[2 * n + 3 : 3 * n + 3]
    tops, dens = refs[3 * n + 3 :]
    c = math.log2(math.e) / math.sqrt(head_dim)
    rows = 2 * q_refs[0].shape[0]
    lane = lax.broadcasted_iota(jnp.int32, (n * rows, head_dim), 1)
    first = (lane == 0).astype(F32).astype(BF16)

    def one_head(h, carry):
        cols = pl.ds(pl.multiple_of(h * head_dim, head_dim), head_dim)
        v = val[:, cols]
        q = jnp.concatenate([r[:, cols] for r in q_refs], axis=0)
        s = nt_dot(
            jnp.concatenate([q, first], axis=1), jnp.concatenate([key[:, cols], bias[...]], axis=1)
        )
        top = jnp.max(s, axis=1, keepdims=True)
        p = jnp.exp2((s - top) * c).astype(BF16)
        o = jnp.dot(
            p, jnp.concatenate([v, jnp.ones_like(v)], axis=1), preferred_element_type=F32
        )
        for j, out in enumerate(outs):
            out[:, cols] = o[j * rows : (j + 1) * rows, :head_dim].astype(out.dtype)
        tops[...] = jnp.where(lane == h, top, tops[...])
        dens[...] = jnp.where(lane == h, o[:, head_dim:], dens[...])
        return carry

    lax.fori_loop(0, HEADS, one_head, 0, unroll=2)
    stats = jnp.zeros((n * rows, head_dim), F32)
    for i, part in enumerate(split3(tops[...]) + split3(dens[...])):
        part = jnp.where(lane < HEADS, part, 0.0)
        stats = stats + (pltpu.roll(part, i * HEADS, 1) if i else part)
    for j, out in enumerate(outs):
        out[:, HEADS * head_dim :] = stats[j * rows : (j + 1) * rows].astype(out.dtype)


def pool(qs, key, val, bias, owned):
    rows, width = qs[0].shape
    n = len(qs) // 2
    head_dim = width // HEADS
    seq = key.shape[0]
    lat = 2 * rows * n
    return pl.pallas_call(
        functools.partial(pool_kernel, n, head_dim),
        in_specs=[VMEM] * (2 * n + 3),
        out_specs=[VMEM] * n,
        out_shape=[
            jax.ShapeDtypeStruct((2 * rows, width + head_dim), F32 if j in owned else BF16)
            for j in range(n)
        ],
        scratch_shapes=[pltpu.VMEM((lat, head_dim), F32)] * 2,
        compiler_params=params(16),
        cost_estimate=pl.CostEstimate(
            flops=12 * lat * seq * width,
            bytes_accessed=2 * (2 * lat * width + 2 * seq * width),
            transcendentals=lat * seq * HEADS,
        ),
        name="pool",
    )(*qs, key, val, bias)


def unite_kernel(chips, head_dim, core, *refs):
    parts = refs[:chips]
    w_all, same, other, pooled, w, sems = refs[chips:]
    width = HEADS * head_dim
    bands = sems.shape[0]
    band = width // bands
    copies = []
    for i in range(bands):
        cut = pl.ds(i * band, band)
        copies.append(pltpu.make_async_copy(w_all.at[core[0], cut], w.at[cut], sems.at[i]))
        copies[-1].start()
    rows = same.shape[0]
    c = math.log2(math.e) / math.sqrt(head_dim)
    stats = [part[:, width:].astype(F32) for part in parts]
    for h in range(HEADS):
        pick = lambda st, i: st[:, i * HEADS + h : i * HEADS + h + 1]
        tops = [pick(st, 0) + pick(st, 1) + pick(st, 2) for st in stats]
        dens = [pick(st, 3) + pick(st, 4) + pick(st, 5) for st in stats]
        top = functools.reduce(jnp.maximum, tops)
        scale = [jnp.exp2((t - top) * c) for t in tops]
        denom = sum(s * d for s, d in zip(scale, dens))
        cols = pl.ds(h * head_dim, head_dim)
        numer = sum(s * part[:, cols].astype(F32) for s, part in zip(scale, parts))
        pooled[:, cols] = (numer / denom).astype(BF16)
    for copy in copies:
        copy.wait()
    t = jnp.dot(pooled[...], w[...], preferred_element_type=F32)
    same[...] = t[:rows]
    other[...] = t[rows:].astype(BF16)


def unite(core, parts, w):
    rows = parts[0].shape[0] // 2
    width = w.shape[1]
    return pl.pallas_call(
        functools.partial(unite_kernel, len(parts), width // HEADS),
        in_specs=[SMEM] + [VMEM] * len(parts) + [HBM],
        out_specs=[VMEM] * 2,
        scratch_shapes=[
            pltpu.VMEM((2 * rows, width), BF16),
            pltpu.VMEM((width, width), BF16),
            pltpu.SemaphoreType.DMA((4,)),
        ],
        out_shape=[
            jax.ShapeDtypeStruct((rows, width), F32),
            jax.ShapeDtypeStruct((rows, width), BF16),
        ],
        compiler_params=params(10),
        name="unite",
    )(core, *parts, w)


def add_kernel(bit, z, a, b, keep, send):
    width = keep.shape[1]
    if width == a.shape[1]:
        keep[...] = a[...] + b[...].astype(F32)
        send[...] = keep[...].astype(BF16)
    else:
        side = (z[0] >> bit) & 1
        for out, at in ((keep, side), (send, 1 - side)):
            cols = pl.ds(pl.multiple_of(at * width, width), width)
            out[...] = (a[:, cols] + b[:, cols].astype(F32)).astype(out.dtype)


def add(z, a, b, bit=None):
    rows, width = a.shape
    width = width if bit is None else width // 2
    return pl.pallas_call(
        functools.partial(add_kernel, bit),
        in_specs=[SMEM, VMEM, VMEM],
        out_specs=[VMEM] * 2,
        out_shape=[
            jax.ShapeDtypeStruct((rows, width), F32),
            jax.ShapeDtypeStruct((rows, width), BF16),
        ],
        compiler_params=params(4),
        name="add",
    )(z, a, b)


def gelu_kernel(a, b, out):
    x = a[...] + b[...].astype(F32)
    out[...] = (0.5 * x * (1.0 + lax.erf(x * math.sqrt(0.5)))).astype(BF16)


def add_gelu(a, b):
    return pl.pallas_call(
        gelu_kernel,
        in_specs=[VMEM] * 2,
        out_specs=VMEM,
        out_shape=jax.ShapeDtypeStruct(a.shape, BF16),
        compiler_params=params(4),
        name="gelu",
    )(a, b)


def join_kernel(bit, z, mine, theirs, out):
    width = mine.shape[1]
    side = (z[0] >> bit) & 1
    for src, at in ((mine, side), (theirs, 1 - side)):
        out[:, pl.ds(pl.multiple_of(at * width, width), width)] = src[...]


def join(z, mine, theirs, bit):
    rows, width = mine.shape
    return pl.pallas_call(
        functools.partial(join_kernel, bit),
        in_specs=[SMEM, VMEM, VMEM],
        out_specs=VMEM,
        out_shape=jax.ShapeDtypeStruct((rows, 2 * width), BF16),
        compiler_params=params(4),
        name="join",
    )(z, mine, theirs)


def decode_kernel(half, head_dim, final, added, chained, n_u, head, dq, tok, *refs):
    refs = list(refs)
    u_refs = [refs.pop(0) for _ in range(n_u)]
    acc_in = refs.pop(0) if added else None
    before = refs.pop(0) if chained else None
    if final:
        meta, out, err, acc = refs
    else:
        out, acc = refs
    c = math.log2(math.e) / math.sqrt(head_dim)
    rows = out.shape[0]
    heads = out.shape[1] // head_dim
    step = min(128, rows)

    def one_head(h, carry):
        cols = pl.ds(pl.multiple_of(h * head_dim, head_dim), head_dim)
        wide = pl.ds(pl.multiple_of((head[0] * heads + h) * head_dim, head_dim), head_dim)
        u = jnp.concatenate([r[:, cols] for r in u_refs], axis=0)
        uu = jnp.concatenate([u, jnp.ones_like(u)], axis=1)
        for r in range(0, rows, step):
            here = pl.ds(half * rows + r, step)
            s = nt_dot(dq[here, wide], u)
            top = jnp.max(s, axis=1, keepdims=True)
            p = jnp.exp2((s - top) * c).astype(BF16)
            o = jnp.dot(p, uu, preferred_element_type=F32)
            dec = (o[:, :head_dim] / o[:, head_dim:]).astype(BF16)
            band = pl.ds(r, step)
            out[band, cols] = dec
            diff = dec.astype(F32) - tok[here, wide].astype(F32)
            start = acc_in[band, :] if added else 0.0
            acc[band, :] = jnp.where(h == 0, start, acc[band, :]) + diff * diff
        return carry

    lax.fori_loop(0, heads, one_head, 0, unroll=2)
    if final:
        valid = (meta[:, half * rows : (half + 1) * rows] >= FLAG).astype(F32)
        valid = jnp.broadcast_to(valid, (8, rows))
        total = jnp.dot(
            valid, acc[...], precision=lax.Precision.HIGHEST, preferred_element_type=F32
        )
        total = jnp.sum(total, axis=1, keepdims=True) * (1.0 / tok.shape[1])
        count = jnp.sum(valid, axis=1, keepdims=True)
        row = lax.broadcasted_iota(jnp.int32, err.shape, 0)
        sums = jnp.where(row == 0, total, count)
        err[...] = sums + before[...] if chained else sums


def decode(half, head, dq, tok, us, acc_in, before, meta):
    rows, width = dq.shape[0] // 2, dq.shape[1]
    head_dim = width // HEADS
    piece = us[0].shape[1]
    lat = len(us) * us[0].shape[0]
    out = jax.ShapeDtypeStruct((rows, piece), BF16)
    acc = jax.ShapeDtypeStruct((rows, head_dim), F32)
    return pl.pallas_call(
        functools.partial(
            decode_kernel, half, head_dim, bool(meta), bool(acc_in), bool(before), len(us)
        ),
        in_specs=[SMEM] + [VMEM] * (2 + len(us) + len(acc_in + before + meta)),
        out_specs=[VMEM] * 2,
        out_shape=[out, jax.ShapeDtypeStruct((8, head_dim), F32) if meta else acc],
        scratch_shapes=[pltpu.VMEM(acc.shape, F32)] if meta else [],
        compiler_params=params(8),
        cost_estimate=pl.CostEstimate(
            flops=6 * rows * lat * piece,
            bytes_accessed=6 * rows * piece,
            transcendentals=rows * lat * piece // head_dim,
        ),
        name="decode",
    )(head, dq, tok, *us, *acc_in, *before, *meta)


def place_kernel(n, core, head, *refs):
    mine, back, out, sem = refs[:n], refs[n : 2 * n], refs[2 * n], refs[2 * n + 1]
    copies = []
    for i in range(n):
        for src, at in ((mine[i], core[0]), (back[i], 1 - core[0])):
            width = src.shape[1]
            cols = pl.ds(pl.multiple_of((head[0] ^ i) * width, width), width)
            copies.append(
                pltpu.make_async_copy(src, out.at[at, :, cols], sem.at[len(copies)])
            )
            copies[-1].start()
    for copy in copies:
        copy.wait()


def place(core, head, mine, back):
    rows, width = mine[0].shape
    n = len(mine)
    return pl.pallas_call(
        functools.partial(place_kernel, n),
        in_specs=[SMEM, SMEM] + [VMEM] * (2 * n),
        out_specs=HBM,
        out_shape=jax.ShapeDtypeStruct((2, rows, n * width), BF16),
        scratch_shapes=[pltpu.SemaphoreType.DMA((2 * n,))],
        compiler_params=params(4),
        cost_estimate=pl.CostEstimate(
            flops=0, bytes_accessed=8 * n * rows * width, transcendentals=0
        ),
        name="place",
    )(core, head, *mine, *back)


def finish_kernel(core, mine, theirs, out, ratio):
    ratio[0] = mine[...] / jnp.broadcast_to(mine[1:2, :], mine.shape)
    ratio[1] = theirs[...] / jnp.broadcast_to(theirs[1:2, :], theirs.shape)
    out[core[0]] = ratio[0, 0, 0]
    out[1 - core[0]] = ratio[1, 0, 0]


def finish(core, mine, theirs):
    return pl.pallas_call(
        finish_kernel,
        in_specs=[SMEM, VMEM, VMEM],
        out_specs=SMEM,
        out_shape=jax.ShapeDtypeStruct((2,), F32),
        scratch_shapes=[pltpu.VMEM((2,) + mine.shape, F32)],
        compiler_params=params(4),
        name="finish",
    )(core, mine, theirs)


def per_device(
    nt, zs, tokens, kind_ids, kind_table, present, lengths, latents, w_key, w_value, w_dquery, w_unite
):
    _, rows, _ = tokens.shape
    chips = nt // 2
    hbm = lambda x: pltpu.with_memory_space_constraint(x, pltpu.HBM)
    t = lax.axis_index("tok")
    z = lax.axis_index("mod").astype(jnp.int32)[None]
    core = (t % 2).astype(jnp.int32)
    swap = lambda x, k: lax.ppermute(x, "tok", [(i, i ^ k) for i in range(nt)])
    swap_z = lambda x, k: lax.ppermute(x, "mod", [(i, i ^ k) for i in range(zs)])
    own = lambda x: lax.dynamic_index_in_dim(x, core, 0, keepdims=True)
    alien = lambda x: lax.dynamic_index_in_dim(x, 1 - core, 0, keepdims=True)
    far = sorted(range(chips), key=lambda j: -bin(j).count("1"))

    theirs = swap(tokens, 1)
    lat_own, lat_alien = own(latents)[0], alien(latents)[0]
    got = {}
    for j in far:
        got[j] = [swap(lat_own, 2 * j) if j else lat_own, swap(lat_alien, 2 * j + 1)]
    position = t * rows + jnp.arange(rows, dtype=jnp.int32)
    valid = (present == 1) & (position[None, :] < lengths[:, None])
    meta = kind_ids + FLAG * valid.astype(jnp.int32)
    meta = jnp.concatenate([own(meta), swap(alien(meta), 1)], axis=1)
    one = core[None]
    key, val, bias, hid, tok = project(
        one, hbm(tokens), theirs, meta, hbm(kind_table), hbm(w_key), hbm(w_value)
    )

    near = max(1, chips // 2)
    calls = [[0] + far[: near - 1], [j for j in far[near - 1 :] if j]]
    parts = [None] * chips
    for i, call in enumerate(calls):
        if call:
            qs = [x for j in call for x in got[j]]
            owned = [at for at, j in enumerate(call) if j == 0]
            sums = pool(qs, key, val, bias, owned)
            if i == 0:
                sums, key = lax.optimization_barrier((sums, key))
            for j, s in zip(call, sums):
                parts[j] = swap(s, 2 * j) if j else s
    dq = query(one, hid, hbm(w_dquery))
    parts[far[-2]], dq = lax.optimization_barrier((parts[far[-2]], dq))
    keep, send = unite(one, parts, hbm(w_unite))

    bits = zs.bit_length() - 1
    got_back = swap(send, 1)
    for bit in range(bits):
        keep, send = add(z, keep, got_back, bit if bit + 1 < bits else None)
        got_back = swap_z(send, 1 << bit)
    u = add_gelu(keep, got_back)
    for bit in reversed(range(1, bits - 1)):
        u = join(z, u, swap_z(u, 1 << bit), bit)
    us = [[swap(u, 2 * j) if j else u for j in range(chips)]]
    side = jnp.zeros_like(z)
    if bits > 1:
        side = z & 1
        us.append([swap_z(x, 1) for x in us[0]])
    for i, x in enumerate(us):
        us[i] = x + [swap(y, 1) for y in x]

    n = len(us)
    outs, accs, back = {}, {1: [], 0: []}, []
    err = []
    for i in range(n):
        for half in (1, 0):
            last = i == n - 1
            args = (dq, tok, us[i], accs[half], err if last else [], [meta] if last else [])
            outs[half, i], acc = decode(half, side ^ i, *args)
            accs[half] = [acc]
            if last:
                err = [acc]
        back.append(swap(outs[1, i], 1))
    err = err[0]
    decoded = place(one, side, [outs[0, i] for i in range(n)], back)
    errs = [swap(err, 2 * j) if j else err for j in range(chips)]
    err = sum(errs)
    return decoded, finish(one, err, swap(err, 1))


def solution(mesh):
    nt, zs = mesh.shape["tok"], mesh.shape["mod"]
    in_specs = (
        P("mod", "tok", None),
        P("mod", "tok"),
        P("mod", None, None),
        P("mod", "tok"),
        P("mod"),
        P("mod", "tok", None),
        P("mod", None, None),
        P("mod", None, None),
        P("mod", None, None),
        P("mod", None, None),
    )
    out_specs = (P("mod", "tok", None), P("mod"))


    def body(*args):
        return per_device(nt, zs, *args)

    return jax.shard_map(
        body, mesh=mesh, in_specs=in_specs, out_specs=out_specs, check_vma=False
    )
```
